32 devices in a mesh: face: 2 (over x), patch: 16 (over z, y, core).
Axes of the slice: x: 2, y: 2, z: 4, core: 2. Of those that a mesh axis runs over, the one named last changes fastest.
Arguments:
- features: bfloat16 [32, 2, 65536], P(None, 'face', 'patch'), may hold values from -6 to 6
- film_first: float32 [2, 32], replicated, may hold values from -3 to 3
- weight_first: bfloat16 [32, 288], replicated, may hold values from -0.375 to 0.375
- film_second: float32 [2, 32], replicated, may hold values from -3 to 3
- weight_second: bfloat16 [64, 288], replicated, may hold values from -0.375 to 0.375
- film_third: float32 [2, 64], replicated, may hold values from -3 to 3
- weight_third: bfloat16 [128, 576], replicated, may hold values from -0.25 to 0.25
- film_fourth: float32 [2, 128], replicated, may hold values from -3 to 3
- weight_fourth: bfloat16 [128, 1152], replicated, may hold values from -0.1875 to 0.1875
- film_fifth: float32 [2, 192], replicated, may hold values from -3 to 3
- weight_fifth: bfloat16 [64, 1728], replicated, may hold values from -0.15625 to 0.15625
- film_sixth: float32 [2, 96], replicated, may hold values from -3 to 3
- weight_sixth: bfloat16 [32, 864], replicated, may hold values from -0.21875 to 0.21875
- link_patch: int32 [2, 16, 8], replicated, may hold values from 0 to 15, as said below
- link_shift: int32 [2, 16, 8], replicated, may hold values from -1 to 1, as said below
- link_turn: int32 [2, 16, 8], replicated, may hold values from 0 to 3, as said below
Outputs:
- denoised: bfloat16 [32, 2, 65536], P(None, 'face', 'patch')
The draws below stay inside these ranges and needn't reach their ends.
Inputs may be any that keep to these rules, and one draw needn't show every extreme that they name: `link_patch`: patch p of a face sits at row p // 4 and column p % 4 of a 4 x 4 grid of patches. For a direction that stays inside that grid the entry is the grid neighbour. For a direction that leaves it the entry is a patch on the outer row or column of the neighbouring face's grid such that every cell that padded reads from it lies on that face's outer border. `link_shift`: 0 for a direction that stays inside the face's grid of patches, -1 or +1 for one that leaves it. `link_turn`: 0 for a direction that stays inside the face's grid of patches.
All inputs are finite; a program needn't handle non-finite values.
Results may differ from the reference program's by a relative error of at most 0.009.
Values may be sent and summed in bfloat16 or wider, within the bound.
A program may use at most 128 MiB of HBM per device.

```python
import math
import jax
import jax.numpy as jnp
from jax import lax

C1 = 32
C2 = 64
C3 = 128
PATCH_ROWS = 4
PATCH_COLS = 4
CELLS = 4096
N_FACE = 2
N_PATCH = 16


def link_tables(key):
    table_shape = (N_FACE, N_PATCH, 8)
    patch_ids = jnp.arange(N_PATCH, dtype=jnp.int32)[None, :, None]
    patch_row = patch_ids // PATCH_COLS
    patch_col = patch_ids % PATCH_COLS
    step_row = jnp.array([-1, 1, 0, 0, -1, -1, 1, 1], dtype=jnp.int32)[None, None, :]
    step_col = jnp.array([0, 0, -1, 1, -1, 1, -1, 1], dtype=jnp.int32)[None, None, :]
    near_row = patch_row + step_row
    near_col = patch_col + step_col
    inside = (near_row >= 0) & (near_row < PATCH_ROWS) & (near_col >= 0) & (near_col < PATCH_COLS)
    inside = jnp.broadcast_to(inside, table_shape)
    grid_patch = jnp.broadcast_to(near_row * PATCH_COLS + near_col, table_shape)
    far_side = jax.random.randint(jax.random.fold_in(key, 202), table_shape, 0, 2, dtype=jnp.int32) * 2 - 1
    far_turn = jax.random.randint(jax.random.fold_in(key, 303), table_shape, 0, 4, dtype=jnp.int32)
    read_edge = jnp.broadcast_to(jnp.array([1, 0, 3, 2, 1, 1, 0, 0], dtype=jnp.int32)[None, None, :], table_shape)
    source_of = jnp.array([3, 2, 0, 1], dtype=jnp.int32)
    edge_now = read_edge
    for count in range(1, 4):
        edge_now = jnp.where(far_turn >= count, source_of[edge_now], edge_now)
    pick_row = jax.random.randint(jax.random.fold_in(key, 404), table_shape, 0, PATCH_ROWS, dtype=jnp.int32)
    pick_col = jax.random.randint(jax.random.fold_in(key, 505), table_shape, 0, PATCH_COLS, dtype=jnp.int32)
    far_patch = jnp.where(edge_now == 0, pick_col, jnp.where(edge_now == 1, (PATCH_ROWS - 1) * PATCH_COLS + pick_col, jnp.where(edge_now == 2, pick_row * PATCH_COLS, pick_row * PATCH_COLS + PATCH_COLS - 1)))
    zeros_table = jnp.zeros(table_shape, jnp.int32)
    return (jnp.where(inside, grid_patch, far_patch).astype(jnp.int32), jnp.where(inside, zeros_table, far_side).astype(jnp.int32), jnp.where(inside, zeros_table, far_turn).astype(jnp.int32))


def draw_link_patch(key, part):
    return link_tables(key)[0]


def draw_link_shift(key, part):
    return link_tables(key)[1]


def draw_link_turn(key, part):
    return link_tables(key)[2]


def shard_levels(key, dims, cuts, least, top_value):
    def one(dim, parts):
        draws = jax.random.uniform(jax.random.fold_in(jax.random.fold_in(key, 6), dim), (parts,), jnp.float32, least / len(cuts), top_value / len(cuts))
        return jnp.repeat(jnp.exp(draws), dims[dim] // parts).reshape((-1,) + (1,) * (len(dims) - dim - 1))

    level = one(*cuts[0])
    for cut in cuts[1:]:
        level = level * one(*cut)
    return level


def noise(own_key, shape, spread, limit, split=(), kind=jnp.bfloat16):
    level = shard_levels(own_key, shape, split, -0.22, 0.18) if split else 1.0
    values = jax.random.normal(own_key, shape, jnp.float32) * spread * level
    return jnp.minimum(jnp.maximum(values, -limit), limit).astype(kind)


def setup_inputs(seed: int = 0) -> dict:
    seeds = jax.random.split(jax.random.key(seed), 17)
    return {
        "features": noise(seeds[0], (C1, N_FACE, N_PATCH * CELLS), 1.0, 6.0, ((1, 2), (2, 16))),
        "film_first": noise(seeds[1], (2, C1), 0.5, 3.0, (), jnp.float32),
        "weight_first": noise(seeds[2], (C1, 9 * C1), (9 * C1) ** -0.5, 0.375),
        "film_second": noise(seeds[3], (2, C1), 0.5, 3.0, (), jnp.float32),
        "weight_second": noise(seeds[4], (C2, 9 * C1), (9 * C1) ** -0.5, 0.375),
        "film_third": noise(seeds[5], (2, C2), 0.5, 3.0, (), jnp.float32),
        "weight_third": noise(seeds[6], (C3, 9 * C2), (9 * C2) ** -0.5, 0.25),
        "film_fourth": noise(seeds[7], (2, C3), 0.5, 3.0, (), jnp.float32),
        "weight_fourth": noise(seeds[8], (C3, 9 * C3), (9 * C3) ** -0.5, 0.1875),
        "film_fifth": noise(seeds[9], (2, C3 + C2), 0.5, 3.0, (), jnp.float32),
        "weight_fifth": noise(seeds[10], (C2, 9 * (C3 + C2)), (9 * (C3 + C2)) ** -0.5, 0.15625),
        "film_sixth": noise(seeds[11], (2, C2 + C1), 0.5, 3.0, (), jnp.float32),
        "weight_sixth": noise(seeds[12], (C1, 9 * (C2 + C1)), (9 * (C2 + C1)) ** -0.5, 0.21875),
        "link_patch": draw_link_patch(jax.random.fold_in(seeds[16], 71), 0),
        "link_shift": draw_link_shift(jax.random.fold_in(seeds[16], 71), 0),
        "link_turn": draw_link_turn(jax.random.fold_in(seeds[16], 71), 0),
    }


EPSILON = 1e-05
FLOOR_SQUARE = 0.5

def activate(values, modulation):
    channels = values.shape[-2]
    mean_square = lax.optimization_barrier(jnp.mean(values * values, axis=-2, keepdims=True))
    if channels >= 64:
        inverse = lax.rsqrt(mean_square + EPSILON)
    else:
        inverse = lax.rsqrt(jnp.maximum(mean_square, FLOOR_SQUARE))
    shaped = values * inverse * (1.0 + modulation[0][:, None]) + modulation[1][:, None]
    return jax.nn.silu(shaped).astype(jnp.bfloat16)

def frame_of(grids):
    return jnp.stack([grids[..., 0, :], grids[..., -1, :], grids[..., :, 0], grids[..., :, -1]], axis=-3)

def turn_once(frames):
    return jnp.stack([frames[..., 3, :, :], frames[..., 2, :, :], frames[..., 0, :, ::-1], frames[..., 1, :, ::-1]], axis=-3)

def turned(frames, quarters):
    result = frames
    current = frames
    for count in range(1, 4):
        current = turn_once(current)
        result = jnp.where((quarters == count)[:, None, None, None], current, result)
    return result

def cycle_of(frames):
    edges = jnp.stack([frames[0, 1], frames[1, 0], frames[2, 3], frames[3, 2]])
    corners = jnp.stack([frames[4, 1, :, -1], frames[5, 1, :, 0], frames[6, 0, :, -1], frames[7, 0, :, 0]])
    return (edges, corners)

def assemble(grid, edges, corners):
    middle = jnp.concatenate([edges[2][:, :, None], grid, edges[3][:, :, None]], axis=2)
    upper = jnp.concatenate([corners[0][:, None], edges[0], corners[1][:, None]], axis=1)
    lowest = jnp.concatenate([corners[2][:, None], edges[1], corners[3][:, None]], axis=1)
    return jnp.concatenate([upper[:, None, :], middle, lowest[:, None, :]], axis=1)

def stencil(padded, weight):
    channels = padded.shape[0]
    length = padded.shape[1] - 2
    columns = [padded[:, row_start:row_start + length, col_start:col_start + length].reshape(channels, length * length) for row_start in range(3) for col_start in range(3)]
    return jnp.dot(weight, jnp.concatenate(columns, axis=0), preferred_element_type=jnp.float32)

def level_conv(active, weight, tables):
    link_patch, link_shift, link_turn = tables
    face_count, patch_count, channels, cells = active.shape
    length = math.isqrt(cells)
    grids = active.reshape(face_count, patch_count, channels, length, length)
    frames = frame_of(grids)

    def one_patch(position):
        face_id = position // patch_count
        patch_id = position % patch_count
        source_face = jnp.mod(face_id + link_shift[face_id, patch_id], face_count)
        neighbours = frames[source_face, link_patch[face_id, patch_id]]
        edges, corners = cycle_of(turned(neighbours, link_turn[face_id, patch_id]))
        return stencil(assemble(grids[face_id, patch_id], edges, corners), weight)
    result = lax.map(one_patch, jnp.arange(face_count * patch_count, dtype=jnp.int32))
    return result.reshape(face_count, patch_count, weight.shape[0], cells)

def coarsen(field):
    leading = field.shape[:-1]
    length = math.isqrt(field.shape[-1])
    half_side = length // 2
    blocks = field.reshape(leading + (half_side, 2, half_side, 2))
    return lax.optimization_barrier(jnp.mean(blocks, axis=(-3, -1))).reshape(leading + (half_side * half_side,))

def refine(field):
    leading = field.shape[:-1]
    length = math.isqrt(field.shape[-1])
    grid = field.reshape(leading + (length, length))
    grid = jnp.repeat(jnp.repeat(grid, 2, axis=-2), 2, axis=-1)
    return grid.reshape(leading + (4 * length * length,))

def reference(features, film_first, weight_first, film_second, weight_second, film_third, weight_third, film_fourth, weight_fourth, film_fifth, weight_fifth, film_sixth, weight_sixth, link_patch, link_shift, link_turn):
    tables = (link_patch, link_shift, link_turn)
    fine = features.reshape(C1, N_FACE, N_PATCH, CELLS).transpose(1, 2, 0, 3).astype(jnp.float32)
    first = fine + level_conv(activate(fine, film_first), weight_first, tables)
    skip_fine = first.astype(jnp.bfloat16)
    second = level_conv(activate(coarsen(first), film_second), weight_second, tables)
    skip_middle = second.astype(jnp.bfloat16)
    third = level_conv(activate(coarsen(second), film_third), weight_third, tables)
    fourth = third + level_conv(activate(third, film_fourth), weight_fourth, tables)
    joined_middle = jnp.concatenate([refine(fourth), skip_middle.astype(jnp.float32)], axis=-2)
    fifth = level_conv(activate(joined_middle, film_fifth), weight_fifth, tables)
    joined_fine = jnp.concatenate([refine(fifth), skip_fine.astype(jnp.float32)], axis=-2)
    result = skip_fine.astype(jnp.float32) + level_conv(activate(joined_fine, film_sixth), weight_sixth, tables)
    result = result.astype(jnp.bfloat16)
    return result.transpose(2, 0, 1, 3).reshape(C1, N_FACE, N_PATCH * CELLS)
```

```python
import functools
import math

import jax
import jax.numpy as jnp
from jax import lax
from jax.experimental import pallas as pl
from jax.experimental.pallas import tpu as pltpu
from jax.sharding import PartitionSpec as P

EPSILON = 1e-05
FLOOR_SQUARE = 0.5
MESH = pl.DeviceIdType.MESH
F32 = jnp.float32
BF16 = jnp.bfloat16

STEPS = ((-1, 0), (1, 0), (0, -1), (0, 1), (-1, -1), (-1, 1), (1, -1), (1, 1))
OPPOSITE = (1, 0, 3, 2, 7, 6, 5, 4)
READ_EDGE = (1, 0, 3, 2, 1, 1, 0, 0)
READ_LAST = (None, None, None, None, 1, 0, 1, 0)
SIDE_GAP = 8


def turned_source(edge, turns):
    flip = 0
    for _ in range(turns):
        if edge >= 2:
            flip ^= 1
        edge = (3, 2, 0, 1)[edge]
    return edge, flip


def corner_cell(direction, turns):
    edge, flip = turned_source(READ_EDGE[direction], turns)
    last = READ_LAST[direction] ^ flip
    return ((0, last), (1, last), (last, 0), (last, 1))[edge]


def pick(index, options):
    result = jnp.int32(options[0])
    for count in range(1, len(options)):
        result = jnp.where(index == count, jnp.int32(options[count]), result)
    return result


def grid_of(patches):
    rows = 1 << ((patches.bit_length() - 1) // 2)
    return rows, patches // rows


def pack_of(length, channels):
    return max(1, min(length // 16, 128 // channels))


def rim_shape(length, channels):
    count = pack_of(length, channels)
    return (length // count, channels * count)


def pack(edge):
    length, channels = edge.shape
    count = pack_of(length, channels)
    if count == 1:
        return edge
    step = length // count
    return jnp.concatenate([edge[i * step : (i + 1) * step] for i in range(count)], axis=1)


def unpack(rim, length, channels):
    count = pack_of(length, channels)
    if count == 1:
        return rim
    return jnp.concatenate([rim[:, i * channels : (i + 1) * channels] for i in range(count)], axis=0)


def activated(parts, films):
    channels = sum(part.shape[1] for part in parts)
    total = sum(jnp.sum(part * part, axis=1, keepdims=True) for part in parts)
    mean_square = total * (1.0 / channels)
    if channels >= 64:
        inverse = lax.rsqrt(mean_square + EPSILON)
    else:
        inverse = lax.rsqrt(jnp.maximum(mean_square, FLOOR_SQUARE))
    results = []
    for part, (scale, shift) in zip(parts, films):
        shaped = part * inverse * scale + shift
        results.append(shaped / (1.0 + jnp.exp(-shaped)))
    return results


def kernel(faces, patches, sizes, *refs):
    rows, cols = grid_of(patches)
    slots = 2 * (rows + cols)
    outers = 2 * cols + 2 * (rows - 2)
    shifts = 1 if faces == 2 else 2
    side, c1, c2, c3 = sizes
    mid, low = side // 2, side // 4
    (feat, f1, f2, f3, f4, f5, f6, w1, w2, w3, w4, w5, w6, link_patch, link_shift, link_turn, out) = refs[:17]
    scratch = refs[17:]
    p1, p2a, p2b, p3, keep1, keep2, keep3, up2, up1 = scratch[:9]
    rims, landed = scratch[9:15], scratch[15:21]
    near_send, far_send, recv = scratch[21:]

    face = lax.axis_index("face")
    me = lax.axis_index("patch")
    row, col = me // cols, me % cols
    top, bottom, left, right = row == 0, row == rows - 1, col == 0, col == cols - 1
    upright, across = jnp.logical_or(top, bottom), jnp.logical_or(left, right)
    outer = jnp.logical_or(upright, across)
    inside = []
    for dr, dc in STEPS:
        r, c = row + dr, col + dc
        inside.append(
            jnp.logical_and(
                jnp.logical_and(r >= 0, r < rows), jnp.logical_and(c >= 0, c < cols)
            )
        )

    def outer_patch(k):
        m = k - 2 * cols
        middle = (1 + m // 2) * cols + (m % 2) * (cols - 1)
        return jnp.where(k < cols, k, jnp.where(k < 2 * cols, (rows - 2) * cols + k, middle))

    def far_face(s):
        return lax.rem(face + (faces - 1 if s == 0 else 1), faces)

    barrier = pltpu.get_barrier_semaphore()
    for d, (dr, dc) in enumerate(STEPS):

        @pl.when(inside[d])
        def _(dr=dr, dc=dc):
            pl.semaphore_signal(
                barrier, inc=1, device_id=(face, me + dr * cols + dc), device_id_type=MESH
            )

    @pl.when(outer)
    def _():
        for s in range(shifts):

            def greet(k, carry, s=s):
                pl.semaphore_signal(
                    barrier, inc=1, device_id=(far_face(s), outer_patch(k)), device_id_type=MESH
                )
                return carry

            lax.fori_loop(0, outers, greet, 0)

    def meet():
        peers = sum(jnp.where(there, 1, 0) for there in inside)
        pl.semaphore_wait(barrier, peers + jnp.where(outer, outers * shifts, 0))

    where_from = []
    for d in range(8):
        q = link_patch[face, me, d]
        shift = link_shift[face, me, d]
        turn = link_turn[face, me, d]
        q_row, q_col = q // cols, q % cols
        if d < 4:
            edge = pick(turn, [turned_source(READ_EDGE[d], t)[0] for t in range(4)])
            flip = pick(turn, [turned_source(READ_EDGE[d], t)[1] for t in range(4)])
        else:
            last_row = pick(turn, [corner_cell(d, t)[0] for t in range(4)])
            last_col = pick(turn, [corner_cell(d, t)[1] for t in range(4)])
            on_row = q_row == last_row * (rows - 1)
            edge = jnp.where(on_row, last_row, 2 + last_col)
            flip = jnp.where(on_row, last_col, last_row)
            flip = jnp.where(shift == 0, jnp.int32(READ_LAST[d]), flip)
        slot = jnp.where(
            edge == 0,
            q_col,
            jnp.where(
                edge == 1,
                cols + q_col,
                jnp.where(edge == 2, 2 * cols + q_row, 2 * cols + rows + q_row),
            ),
        )
        group = jnp.where(shift < 0, slots, 0) if shifts == 2 else 0
        where_from.append((jnp.where(shift == 0, d, 8 + group + slot), flip))

    def sends(n, act):
        rim, land = rims[n], landed[n]
        for d, (dr, dc) in enumerate(STEPS):
            o = OPPOSITE[d]

            @pl.when(inside[d])
            def _(d=d, dr=dr, dc=dc, o=o):
                act(
                    pltpu.make_async_remote_copy(
                        src_ref=rim.at[READ_EDGE[o]],
                        dst_ref=land.at[o],
                        send_sem=near_send.at[d],
                        recv_sem=recv.at[n, o],
                        device_id=(face, me + dr * cols + dc),
                        device_id_type=MESH,
                    )
                )

        mine = (
            (upright, jnp.where(top, 0, 1), jnp.where(top, col, cols + col)),
            (across, jnp.where(left, 2, 3), jnp.where(left, 2 * cols + row, 2 * cols + rows + row)),
        )
        for way, (present, edge, slot) in enumerate(mine):

            @pl.when(present)
            def _(way=way, edge=edge, slot=slot):
                for s in range(shifts):

                    def one(k, carry, s=s):
                        place = 8 + s * slots + slot
                        act(
                            pltpu.make_async_remote_copy(
                                src_ref=rim.at[edge],
                                dst_ref=land.at[place],
                                send_sem=far_send.at[way, s, k],
                                recv_sem=recv.at[n, place],
                                device_id=(far_face(s), outer_patch(k)),
                                device_id_type=MESH,
                            )
                        )
                        return carry

                    lax.fori_loop(0, outers, one, 0)

    def arrive(n):
        rim, land = rims[n], landed[n]

        def wait(place):
            pltpu.make_async_remote_copy(
                src_ref=rim.at[0],
                dst_ref=land.at[place],
                send_sem=near_send.at[0],
                recv_sem=recv.at[n, place],
                device_id=(face, me),
                device_id_type=MESH,
            ).wait_recv()

        for d in range(8):

            @pl.when(inside[d])
            def _(d=d):
                wait(d)

        @pl.when(outer)
        def _():
            def one(k, carry):
                wait(8 + k)
                return carry

            lax.fori_loop(0, slots * shifts, one, 0)

    def exchange(n, length, fields):
        pitch = length + 2 * SIDE_GAP
        channels = sum(count for _, count in fields)
        starts = (
            pl.ds(pitch + SIDE_GAP, length),
            pl.ds(length * pitch + SIDE_GAP, length),
            pl.ds(pitch + SIDE_GAP, length, pitch),
            pl.ds(pitch + SIDE_GAP + length - 1, length, pitch),
        )
        for e, span in enumerate(starts):
            pieces = [ref[span, :][:, :count].astype(BF16) for ref, count in fields]
            edge = pieces[0] if len(pieces) == 1 else jnp.concatenate(pieces, axis=1)
            rims[n][e] = pack(edge)
        if n == 0:
            meet()
        sends(n, lambda copy: copy.start())
        arrive(n)
        line = lax.broadcasted_iota(jnp.int32, (length, length), 0)
        cell = lax.broadcasted_iota(jnp.int32, (length, length), 1)
        targets = (
            pl.ds(SIDE_GAP, length),
            pl.ds((length + 1) * pitch + SIDE_GAP, length),
            pl.ds(pitch + SIDE_GAP - 1, length, pitch),
            pl.ds(pitch + SIDE_GAP + length, length, pitch),
            pl.ds(SIDE_GAP - 1, 1),
            pl.ds(SIDE_GAP + length, 1),
            pl.ds((length + 1) * pitch + SIDE_GAP - 1, 1),
            pl.ds((length + 1) * pitch + SIDE_GAP + length, 1),
        )
        for d in range(8):
            place, flip = where_from[d]
            edge = unpack(landed[n][place], length, channels)
            if d < 4:
                order = jnp.where(cell == line + flip * (length - 1 - 2 * line), 1.0, 0.0)
                value = jnp.dot(order.astype(BF16), edge, preferred_element_type=F32)
            else:
                wide = edge.astype(F32)
                value = jnp.where(flip == 1, wide[length - 1 :], wide[:1])
            start = 0
            for ref, count in fields:
                piece = value[:, start : start + count]
                if count < 128:
                    piece = jnp.concatenate(
                        [piece, jnp.zeros((piece.shape[0], 128 - count), F32)], axis=1
                    )
                ref[targets[d], :] = piece
                start += count
        sends(n, lambda copy: copy.wait_send())

    def put(ref, base, length, count, values):
        pitch = length + 2 * SIDE_GAP
        for i in range(values.shape[0] // length):
            start = pl.multiple_of(base * pitch, 8) + (i + 1) * pitch + SIDE_GAP
            ref[pl.ds(start, length), :count] = values[i * length : (i + 1) * length]

    def conv(base, step, length, fields):
        pitch = length + 2 * SIDE_GAP
        total = None
        for ref, count, weight in fields:
            for u in range(3):
                for v in range(3):
                    lines = []
                    for i in range(step):
                        start = pl.multiple_of(base * pitch, 8) + (i + u) * pitch + SIDE_GAP - 1 + v
                        lines.append(ref[pl.ds(start, length), :][:, :count].astype(BF16))
                    block = lines[0] if step == 1 else jnp.concatenate(lines, axis=0)
                    term = lax.dot_general(
                        block,
                        weight[3 * u + v],
                        (((1,), (1,)), ((), ())),
                        preferred_element_type=F32,
                    )
                    total = term if total is None else total + term
        return total

    def film_of(ref, start, count):
        return (1.0 + ref[0:1, start : start + count], ref[1:2, start : start + count])

    def loop(count, body):
        def run(i, carry):
            body(i)
            return carry

        lax.fori_loop(0, count, run, 0)

    def coarse(ref, base, step, length, count):
        half = length // 2
        lines = []
        for i in range(step):
            start = pl.multiple_of(base * 2 * length, 8) + 2 * i * length
            quad = [
                ref[pl.ds(start + a * length + b, half, 2), :][:, :count]
                for a in range(2)
                for b in range(2)
            ]
            lines.append((quad[0] + quad[1] + (quad[2] + quad[3])) * 0.25)
        return lines[0] if step == 1 else jnp.concatenate(lines, axis=0)

    def spread(ref, base, step, length, values):
        for i in range(step):
            line = values[i * length : (i + 1) * length]
            start = pl.multiple_of(base * 4 * length, 8) + 4 * i * length
            for a in range(2):
                for b in range(2):
                    ref[pl.ds(start + 2 * a * length + b, length, 2), :] = line

    def lanes(values):
        count = values.shape[1]
        if count == 128:
            return values
        return jnp.concatenate([values, jnp.zeros((values.shape[0], 128 - count), F32)], axis=1)

    step = 8
    cells = step * side
    film1 = film_of(f1, 0, c1)

    def enter(i):
        start = pl.multiple_of(i * cells, cells)
        values = feat[:, pl.ds(start, cells)].astype(F32).T
        keep1[pl.ds(start, cells), :c1] = values
        put(p1, i * step, side, c1, activated([values], [film1])[0])

    loop(side // step, enter)
    exchange(0, side, [(p1, c1)])

    def first(i):
        start = pl.multiple_of(i * cells, cells)
        values = conv(i * step, step, side, [(p1, c1, w1)])
        keep1[pl.ds(start, cells), :c1] = keep1[pl.ds(start, cells), :c1] + values

    loop(side // step, first)

    step2 = 8
    cells2 = step2 * mid
    film2 = film_of(f2, 0, c1)

    def shrink(i):
        values = coarse(keep1, i * step2, step2, side, c1)
        put(p2a, i * step2, mid, c1, activated([values], [film2])[0])

    loop(mid // step2, shrink)
    exchange(1, mid, [(p2a, c1)])

    def second(i):
        start = pl.multiple_of(i * cells2, cells2)
        keep2[pl.ds(start, cells2), :c2] = conv(i * step2, step2, mid, [(p2a, c1, w2)])

    loop(mid // step2, second)

    put(p3, 0, low, c2, activated([coarse(keep2, 0, low, mid, c2)], [film_of(f3, 0, c2)])[0])
    exchange(2, low, [(p3, c2)])
    keep3[...] = conv(0, low, low, [(p3, c2, w3)])
    put(p3, 0, low, c3, activated([keep3[...]], [film_of(f4, 0, c3)])[0])
    exchange(3, low, [(p3, c3)])
    spread(up2, 0, low, low, keep3[...] + conv(0, low, low, [(p3, c3, w4)]))

    films5 = [film_of(f5, 0, c3), film_of(f5, c3, c2)]

    def join_middle(i):
        start = pl.multiple_of(i * cells2, cells2)
        skip = keep2[pl.ds(start, cells2), :c2].astype(BF16).astype(F32)
        one, two = activated([up2[pl.ds(start, cells2), :], skip], films5)
        put(p2a, i * step2, mid, c3, one)
        put(p2b, i * step2, mid, c2, two)

    loop(mid // step2, join_middle)
    exchange(4, mid, [(p2a, c3), (p2b, c2)])

    def fifth(i):
        values = conv(
            i * step2,
            step2,
            mid,
            [(p2a, c3, w5.at[:, :, :c3]), (p2b, c2, w5.at[:, :, c3:])],
        )
        spread(up1, i * step2, step2, mid, lanes(values))

    loop(mid // step2, fifth)

    film6 = [film_of(f6, 0, c2 + c1)]

    def join_fine(i):
        start = pl.multiple_of(i * cells, cells)
        skip = keep1[pl.ds(start, cells), :c1].astype(BF16).astype(F32)
        values = jnp.concatenate([up1[pl.ds(start, cells), :c2], skip], axis=1)
        put(p1, i * step, side, c2 + c1, activated([values], film6)[0])

    loop(side // step, join_fine)
    exchange(5, side, [(p1, c2 + c1)])

    def last(i):
        start = pl.multiple_of(i * cells, cells)
        skip = keep1[pl.ds(start, cells), :c1].astype(BF16).astype(F32)
        values = skip + conv(i * step, step, side, [(p1, c2 + c1, w6)])
        out[:, pl.ds(start, cells)] = values.T.astype(BF16)

    loop(side // step, last)


def body(faces, patches, features, f1, w1, f2, w2, f3, w3, f4, w4, f5, w5, f6, w6, *tables):
    c1, _, count = features.shape
    c2, c3 = w2.shape[0], w3.shape[0]
    side = math.isqrt(count)
    mid, low = side // 2, side // 4
    rows, cols = grid_of(patches)
    slots = 2 * (rows + cols)
    outers = 2 * cols + 2 * (rows - 2)
    shifts = 1 if faces == 2 else 2
    places = 8 + slots * shifts

    def taps(weight):
        return weight.reshape(weight.shape[0], 9, -1).transpose(1, 0, 2)

    def padded(length):
        return pltpu.VMEM(((length + 2) * (length + 2 * SIDE_GAP), 128), F32)

    shapes = [
        rim_shape(side, c1),
        rim_shape(mid, c1),
        rim_shape(low, c2),
        rim_shape(low, c3),
        rim_shape(mid, c3 + c2),
        rim_shape(side, c2 + c1),
    ]
    vmem = pl.BlockSpec(memory_space=pltpu.VMEM)
    smem = pl.BlockSpec(memory_space=pltpu.SMEM)
    result = pl.pallas_call(
        functools.partial(kernel, faces, patches, (side, c1, c2, c3)),
        out_shape=jax.ShapeDtypeStruct((c1, count), BF16),
        in_specs=[vmem] * 13 + [smem] * 3,
        out_specs=vmem,
        scratch_shapes=[
            padded(side),
            padded(mid),
            padded(mid),
            padded(low),
            pltpu.VMEM((count, 128), F32),
            pltpu.VMEM((count // 4, 128), F32),
            pltpu.VMEM((count // 16, 128), F32),
            pltpu.VMEM((count // 4, 128), F32),
            pltpu.VMEM((count, 128), F32),
        ]
        + [pltpu.VMEM((4,) + shape, BF16) for shape in shapes]
        + [pltpu.VMEM((places,) + shape, BF16) for shape in shapes]
        + [
            pltpu.SemaphoreType.DMA((8,)),
            pltpu.SemaphoreType.DMA((2, shifts, outers)),
            pltpu.SemaphoreType.DMA((6, places)),
        ],
        compiler_params=pltpu.CompilerParams(
            collective_id=0, has_side_effects=True, vmem_limit_bytes=56 * 1024 * 1024
        ),
    )(
        features[:, 0, :],
        f1, f2, f3, f4, f5, f6,
        taps(w1), taps(w2), taps(w3), taps(w4), taps(w5), taps(w6),
        *tables,
    )
    return result[:, None, :]


def solution(mesh):
    spec = P(None, "face", "patch")
    return jax.shard_map(
        functools.partial(body, mesh.shape["face"], mesh.shape["patch"]),
        mesh=mesh,
        in_specs=(spec,) + (P(),) * 15,
        out_specs=spec,
        check_vma=False,
    )
```

```python
import functools
import math

import jax
import jax.numpy as jnp
from jax import lax
from jax.experimental import pallas as pl
from jax.experimental.pallas import tpu as pltpu
from jax.sharding import PartitionSpec as P

EPSILON = 1e-05
FLOOR_SQUARE = 0.5
MESH = pl.DeviceIdType.MESH
F32 = jnp.float32
BF16 = jnp.bfloat16

STEPS = ((-1, 0), (1, 0), (0, -1), (0, 1), (-1, -1), (-1, 1), (1, -1), (1, 1))
OPPOSITE = (1, 0, 3, 2, 7, 6, 5, 4)
READ_EDGE = (1, 0, 3, 2, 1, 1, 0, 0)
READ_LAST = (None, None, None, None, 1, 0, 1, 0)
SIDE_GAP = 8


def turned_source(edge, turns):
    flip = 0
    for _ in range(turns):
        if edge >= 2:
            flip ^= 1
        edge = (3, 2, 0, 1)[edge]
    return edge, flip


def corner_cell(direction, turns):
    edge, flip = turned_source(READ_EDGE[direction], turns)
    last = READ_LAST[direction] ^ flip
    return ((0, last), (1, last), (last, 0), (last, 1))[edge]


def pick(index, options):
    result = jnp.int32(options[0])
    for count in range(1, len(options)):
        result = jnp.where(index == count, jnp.int32(options[count]), result)
    return result


def grid_of(patches):
    rows = 1 << ((patches.bit_length() - 1) // 2)
    return rows, patches // rows


def pack_of(length, channels):
    return max(1, min(length // 16, 128 // channels))


def rim_shape(length, channels):
    count = pack_of(length, channels)
    return (length // count, channels * count)


def pack(edge):
    length, channels = edge.shape
    count = pack_of(length, channels)
    if count == 1:
        return edge
    step = length // count
    return jnp.concatenate([edge[i * step : (i + 1) * step] for i in range(count)], axis=1)


def unpack(rim, length, channels):
    count = pack_of(length, channels)
    if count == 1:
        return rim
    return jnp.concatenate([rim[:, i * channels : (i + 1) * channels] for i in range(count)], axis=0)


def activated(parts, films):
    channels = sum(part.shape[1] for part in parts)
    total = sum(jnp.sum(part * part, axis=1, keepdims=True) for part in parts)
    mean_square = total * (1.0 / channels)
    if channels >= 64:
        inverse = lax.rsqrt(mean_square + EPSILON)
    else:
        inverse = lax.rsqrt(jnp.maximum(mean_square, FLOOR_SQUARE))
    results = []
    for part, (scale, shift) in zip(parts, films):
        shaped = part * inverse * scale + shift
        results.append(shaped / (1.0 + jnp.exp(-shaped)))
    return results


def kernel(faces, patches, sizes, *refs):
    rows, cols = grid_of(patches)
    slots = 2 * (rows + cols)
    outers = 2 * cols + 2 * (rows - 2)
    shifts = 1 if faces == 2 else 2
    side, c1, c2, c3 = sizes
    mid, low = side // 2, side // 4
    (feat, f1, f2, f3, f4, f5, f6, w1, w2, w3, w4, w5, w6, link_patch, link_shift, link_turn, out) = refs[:17]
    scratch = refs[17:]
    p1, p2a, p2b, p3, keep1, keep2, keep3, up2, up1, mid5, ring, ring_b = scratch[:12]
    t1, t2, t3, t4, t5a, t5b, t6 = scratch[12:19]
    rims, landed = scratch[19:27], scratch[27:35]
    near_send, far_send, recv = scratch[35:]

    face = lax.axis_index("face")
    me = lax.axis_index("patch")
    row, col = me // cols, me % cols
    top, bottom, left, right = row == 0, row == rows - 1, col == 0, col == cols - 1
    upright, across = jnp.logical_or(top, bottom), jnp.logical_or(left, right)
    outer = jnp.logical_or(upright, across)
    inside = []
    for dr, dc in STEPS:
        r, c = row + dr, col + dc
        inside.append(
            jnp.logical_and(
                jnp.logical_and(r >= 0, r < rows), jnp.logical_and(c >= 0, c < cols)
            )
        )

    def outer_patch(k):
        m = k - 2 * cols
        middle = (1 + m // 2) * cols + (m % 2) * (cols - 1)
        return jnp.where(k < cols, k, jnp.where(k < 2 * cols, (rows - 2) * cols + k, middle))

    def far_face(s):
        return lax.rem(face + (faces - 1 if s == 0 else 1), faces)

    barrier = pltpu.get_barrier_semaphore()
    for d, (dr, dc) in enumerate(STEPS):

        @pl.when(inside[d])
        def _(dr=dr, dc=dc):
            pl.semaphore_signal(
                barrier, inc=1, device_id=(face, me + dr * cols + dc), device_id_type=MESH
            )

    @pl.when(outer)
    def _():
        for s in range(shifts):

            def greet(k, carry, s=s):
                pl.semaphore_signal(
                    barrier, inc=1, device_id=(far_face(s), outer_patch(k)), device_id_type=MESH
                )
                return carry

            lax.fori_loop(0, outers, greet, 0)

    def meet():
        peers = sum(jnp.where(there, 1, 0) for there in inside)
        pl.semaphore_wait(barrier, peers + jnp.where(outer, outers * shifts, 0))

    where_from = []
    for d in range(8):
        q = link_patch[face, d, me]
        shift = link_shift[face, d, me]
        turn = link_turn[face, d, me]
        q_row, q_col = q // cols, q % cols
        if d < 4:
            edge = pick(turn, [turned_source(READ_EDGE[d], t)[0] for t in range(4)])
            flip = pick(turn, [turned_source(READ_EDGE[d], t)[1] for t in range(4)])
        else:
            last_row = pick(turn, [corner_cell(d, t)[0] for t in range(4)])
            last_col = pick(turn, [corner_cell(d, t)[1] for t in range(4)])
            on_row = q_row == last_row * (rows - 1)
            edge = jnp.where(on_row, last_row, 2 + last_col)
            flip = jnp.where(on_row, last_col, last_row)
            flip = jnp.where(shift == 0, jnp.int32(READ_LAST[d]), flip)
        slot = jnp.where(
            edge == 0,
            q_col,
            jnp.where(
                edge == 1,
                cols + q_col,
                jnp.where(edge == 2, 2 * cols + q_row, 2 * cols + rows + q_row),
            ),
        )
        group = jnp.where(shift < 0, slots, 0) if shifts == 2 else 0
        where_from.append((jnp.where(shift == 0, d, 8 + group + slot), flip))

    def sends(n, act):
        rim, land, lane = rims[n], landed[n], max(0, n - 5)
        for d, (dr, dc) in enumerate(STEPS):
            o = OPPOSITE[d]

            @pl.when(inside[d])
            def _(d=d, dr=dr, dc=dc, o=o):
                act(
                    pltpu.make_async_remote_copy(
                        src_ref=rim.at[READ_EDGE[o]],
                        dst_ref=land.at[o],
                        send_sem=near_send.at[lane, d],
                        recv_sem=recv.at[n, o],
                        device_id=(face, me + dr * cols + dc),
                        device_id_type=MESH,
                    )
                )

        mine = (
            (upright, jnp.where(top, 0, 1), jnp.where(top, col, cols + col)),
            (across, jnp.where(left, 2, 3), jnp.where(left, 2 * cols + row, 2 * cols + rows + row)),
        )
        for way, (present, edge, slot) in enumerate(mine):

            @pl.when(present)
            def _(way=way, edge=edge, slot=slot):
                for s in range(shifts):

                    def one(k, carry, s=s):
                        place = 8 + s * slots + slot
                        act(
                            pltpu.make_async_remote_copy(
                                src_ref=rim.at[edge],
                                dst_ref=land.at[place],
                                send_sem=far_send.at[lane, way, s, k],
                                recv_sem=recv.at[n, place],
                                device_id=(far_face(s), outer_patch(k)),
                                device_id_type=MESH,
                            )
                        )
                        return carry

                    lax.fori_loop(0, outers, one, 0)

    def arrive(n):
        rim, land = rims[n], landed[n]

        def wait(place):
            pltpu.make_async_remote_copy(
                src_ref=rim.at[0],
                dst_ref=land.at[place],
                send_sem=near_send.at[0, 0],
                recv_sem=recv.at[n, place],
                device_id=(face, me),
                device_id_type=MESH,
            ).wait_recv()

        for d in range(8):

            @pl.when(inside[d])
            def _(d=d):
                wait(d)

        @pl.when(outer)
        def _():
            def one(k, carry):
                wait(8 + k)
                return carry

            lax.fori_loop(0, slots * shifts, one, 0)

    def launch(n, ref, base, pitch, length, count):
        spans = (
            pl.ds(base, length),
            pl.ds(base + (length - 1) * pitch, length),
            pl.ds(base, length, pitch),
            pl.ds(base + length - 1, length, pitch),
        )
        for e, span in enumerate(spans):
            rims[n][e] = pack(ref[span, :][:, :count].astype(BF16))
        if n == 0:
            meet()
        sends(n, lambda copy: copy.start())

    def launch_padded(n, ref, length, count):
        pitch = length + 2 * SIDE_GAP
        launch(n, ref, pitch + SIDE_GAP, pitch, length, count)

    def gather(n, target, source_length, length, channels):
        pitch = length + 2 * SIDE_GAP
        ratio = length // source_length
        line = lax.broadcasted_iota(jnp.int32, (length, source_length), 0) // ratio
        cell = lax.broadcasted_iota(jnp.int32, (length, source_length), 1)
        places = (
            pl.ds(SIDE_GAP, length),
            pl.ds(pitch + SIDE_GAP, length),
            pl.ds(2 * pitch + SIDE_GAP, length),
            pl.ds(3 * pitch + SIDE_GAP, length),
            pl.ds(SIDE_GAP - 1, 1),
            pl.ds(SIDE_GAP + length, 1),
            pl.ds(pitch + SIDE_GAP - 1, 1),
            pl.ds(pitch + SIDE_GAP + length, 1),
        )
        for d in range(8):
            place, flip = where_from[d]
            edge = unpack(landed[n][place], source_length, channels)
            if d < 4:
                order = jnp.where(cell == line + flip * (source_length - 1 - 2 * line), 1.0, 0.0)
                value = jnp.dot(order.astype(BF16), edge, preferred_element_type=F32)
            else:
                wide = edge.astype(F32)
                value = jnp.where(flip == 1, wide[source_length - 1 :], wide[:1])
            target[places[d], :channels] = value

    def border(length, fields, target):
        pitch = length + 2 * SIDE_GAP
        for ref, count, _ in fields:
            for side_base in (2 * pitch, 3 * pitch):
                for end in (SIDE_GAP - 1, SIDE_GAP + length):
                    ref[pl.ds(side_base + end, 1), :count] = jnp.zeros((1, count), F32)
        spots = (
            (0, pl.ds(0, length), (0, 1, 2)),
            (1, pl.ds((length - 1) * length, length), (6, 7, 8)),
            (2, pl.ds(0, length, length), (0, 3, 6)),
            (3, pl.ds(length - 1, length, length), (2, 5, 8)),
        )
        for part, span, taps in spots:
            total = None
            for ref, count, weight in fields:
                for move, tap in enumerate(taps):
                    block = ref[pl.ds(part * pitch + SIDE_GAP - 1 + move, length), :count]
                    term = lax.dot_general(
                        block.astype(BF16),
                        weight[tap],
                        (((1,), (1,)), ((), ())),
                        preferred_element_type=F32,
                    )
                    total = term if total is None else total + term
            target[span, :] = target[span, :] + lanes(total)

    def clear(ref, length):
        pitch = length + 2 * SIDE_GAP
        for start in (0, (length + 1) * pitch):
            ref[pl.ds(start, pitch), :] = jnp.zeros((pitch, 128), F32)
        for start in (SIDE_GAP - 1, SIDE_GAP + length):
            ref[pl.ds(pitch + start, length, pitch), :] = jnp.zeros((length, 128), F32)

    def cut(weight, parts):
        width = weight.shape[1] // 9
        start = 0
        for target in parts:
            count = target.shape[2]
            for k in range(9):
                target[k] = weight[:, k * width + start : k * width + start + count]
            start += count

    def finish(n):
        sends(n, lambda copy: copy.wait_send())

    def put(ref, base, length, count, values):
        pitch = length + 2 * SIDE_GAP
        for i in range(values.shape[0] // length):
            start = pl.multiple_of(base * pitch, 8) + (i + 1) * pitch + SIDE_GAP
            ref[pl.ds(start, length), :count] = values[i * length : (i + 1) * length]

    def conv(base, step, length, fields):
        pitch = length + 2 * SIDE_GAP
        total = None
        for ref, count, weight in fields:
            for u in range(3):
                for v in range(3):
                    lines = []
                    for i in range(step):
                        start = pl.multiple_of(base * pitch, 8) + (i + u) * pitch + SIDE_GAP - 1 + v
                        lines.append(ref[pl.ds(start, length), :][:, :count].astype(BF16))
                    block = lines[0] if step == 1 else jnp.concatenate(lines, axis=0)
                    term = lax.dot_general(
                        block,
                        weight[3 * u + v],
                        (((1,), (1,)), ((), ())),
                        preferred_element_type=F32,
                    )
                    total = term if total is None else total + term
        return total

    def film_of(ref, start, count):
        return (1.0 + ref[0:1, start : start + count], ref[1:2, start : start + count])

    def loop(count, body):
        def run(i, carry):
            body(i)
            return carry

        lax.fori_loop(0, count, run, 0)

    def coarse(ref, base, step, length, count):
        half = length // 2
        lines = []
        for i in range(step):
            start = pl.multiple_of(base * 2 * length, 8) + 2 * i * length
            quad = [
                ref[pl.ds(start + a * length + b, half, 2), :][:, :count]
                for a in range(2)
                for b in range(2)
            ]
            lines.append((quad[0] + quad[1] + (quad[2] + quad[3])) * 0.25)
        return lines[0] if step == 1 else jnp.concatenate(lines, axis=0)

    def spread(ref, base, step, length, values):
        for i in range(step):
            line = values[i * length : (i + 1) * length]
            start = pl.multiple_of(base * 4 * length, 8) + 4 * i * length
            for a in range(2):
                for b in range(2):
                    ref[pl.ds(start + 2 * a * length + b, length, 2), :] = line

    def lanes(values):
        count = values.shape[1]
        if count == 128:
            return values
        return jnp.concatenate([values, jnp.zeros((values.shape[0], 128 - count), F32)], axis=1)

    step = 8
    cells = step * side
    film1 = film_of(f1, 0, c1)

    def enter(i):
        start = pl.multiple_of(i * cells, cells)
        values = feat[:, pl.ds(start, cells)].astype(F32).T
        keep1[pl.ds(start, cells), :c1] = values
        put(p1, i * step, side, c1, activated([values], [film1])[0])

    loop(side // step, enter)
    launch_padded(0, p1, side, c1)
    clear(p1, side)
    cut(w1, [t1])

    def first(i):
        start = pl.multiple_of(i * cells, cells)
        values = conv(i * step, step, side, [(p1, c1, t1)])
        keep1[pl.ds(start, cells), :c1] = keep1[pl.ds(start, cells), :c1] + values

    loop(side // step, first)
    clear(p2a, mid)
    clear(p2b, mid)
    clear(p3, low)
    cut(w2, [t2])
    cut(w3, [t3])
    arrive(0)
    gather(0, ring, side, side, c1)
    border(side, [(ring, c1, t1)], keep1)
    finish(0)

    step2 = 8
    cells2 = step2 * mid
    film2 = film_of(f2, 0, c1)

    def shrink(i):
        values = coarse(keep1, i * step2, step2, side, c1)
        put(p2a, i * step2, mid, c1, activated([values], [film2])[0])

    loop(mid // step2, shrink)
    launch_padded(1, p2a, mid, c1)
    launch(6, keep1, 0, side, side, c1)

    def second(i):
        start = pl.multiple_of(i * cells2, cells2)
        keep2[pl.ds(start, cells2), :c2] = conv(i * step2, step2, mid, [(p2a, c1, t2)])

    loop(mid // step2, second)
    cut(w4, [t4])
    arrive(1)
    gather(1, ring, mid, mid, c1)
    border(mid, [(ring, c1, t2)], keep2)
    finish(1)

    put(p3, 0, low, c2, activated([coarse(keep2, 0, low, mid, c2)], [film_of(f3, 0, c2)])[0])
    launch_padded(2, p3, low, c2)
    launch(7, keep2, 0, mid, mid, c2)
    keep3[...] = conv(0, low, low, [(p3, c2, t3)])
    cut(w5, [t5a, t5b])
    arrive(2)
    gather(2, ring, low, low, c2)
    border(low, [(ring, c2, t3)], keep3)
    finish(2)

    put(p3, 0, low, c3, activated([keep3[...]], [film_of(f4, 0, c3)])[0])
    launch_padded(3, p3, low, c3)
    keep3[...] = keep3[...] + conv(0, low, low, [(p3, c3, t4)])
    cut(w6, [t6])
    arrive(3)
    gather(3, ring, low, low, c3)
    border(low, [(ring, c3, t4)], keep3)
    finish(3)

    launch(4, keep3, 0, low, low, c3)
    spread(up2, 0, low, low, keep3[...])
    films5 = [film_of(f5, 0, c3), film_of(f5, c3, c2)]

    def join_middle(i):
        start = pl.multiple_of(i * cells2, cells2)
        skip = keep2[pl.ds(start, cells2), :c2].astype(BF16).astype(F32)
        one, two = activated([up2[pl.ds(start, cells2), :], skip], films5)
        put(p2a, i * step2, mid, c3, one)
        put(p2b, i * step2, mid, c2, two)

    loop(mid // step2, join_middle)

    def fifth(i):
        start = pl.multiple_of(i * cells2, cells2)
        mid5[pl.ds(start, cells2), :c2] = conv(
            i * step2, step2, mid, [(p2a, c3, t5a), (p2b, c2, t5b)]
        )

    loop(mid // step2, fifth)
    arrive(7)
    arrive(4)
    gather(7, ring_b, mid, mid, c2)
    gather(4, ring, low, mid, c3)
    extent = pl.ds(0, 4 * (mid + 2 * SIDE_GAP))
    one, two = activated([ring[extent, :], ring_b[extent, :c2]], films5)
    ring[extent, :] = one
    ring_b[extent, :c2] = two
    border(mid, [(ring, c3, t5a), (ring_b, c2, t5b)], mid5)
    finish(7)
    finish(4)

    launch(5, mid5, 0, mid, mid, c2)

    def widen(i):
        start = pl.multiple_of(i * cells2, cells2)
        spread(up1, i * step2, step2, mid, mid5[pl.ds(start, cells2), :])

    loop(mid // step2, widen)
    film6 = [film_of(f6, 0, c2 + c1)]

    def join_fine(i):
        start = pl.multiple_of(i * cells, cells)
        skip = keep1[pl.ds(start, cells), :c1].astype(BF16).astype(F32)
        values = jnp.concatenate([up1[pl.ds(start, cells), :c2], skip], axis=1)
        put(p1, i * step, side, c2 + c1, activated([values], film6)[0])

    loop(side // step, join_fine)

    def last(i):
        start = pl.multiple_of(i * cells, cells)
        skip = keep1[pl.ds(start, cells), :c1].astype(BF16).astype(F32)
        keep1[pl.ds(start, cells), :c1] = skip + conv(i * step, step, side, [(p1, c2 + c1, t6)])

    loop(side // step, last)
    arrive(6)
    arrive(5)
    gather(6, ring_b, side, side, c1)
    gather(5, ring, mid, side, c2)
    extent = pl.ds(0, 4 * (side + 2 * SIDE_GAP))
    values = jnp.concatenate([ring[extent, :c2], ring_b[extent, :c1]], axis=1)
    ring[extent, : c2 + c1] = activated([values], film6)[0]
    border(side, [(ring, c2 + c1, t6)], keep1)

    def leave(i):
        start = pl.multiple_of(i * cells, cells)
        out[:, pl.ds(start, cells)] = keep1[pl.ds(start, cells), :c1].T.astype(BF16)

    loop(side // step, leave)
    finish(6)
    finish(5)


def body(faces, patches, features, f1, w1, f2, w2, f3, w3, f4, w4, f5, w5, f6, w6, *tables):
    c1, _, count = features.shape
    c2, c3 = w2.shape[0], w3.shape[0]
    side = math.isqrt(count)
    mid, low = side // 2, side // 4
    rows, cols = grid_of(patches)
    slots = 2 * (rows + cols)
    outers = 2 * cols + 2 * (rows - 2)
    shifts = 1 if faces == 2 else 2
    places = 8 + slots * shifts

    def padded(length):
        return pltpu.VMEM(((length + 2) * (length + 2 * SIDE_GAP), 128), F32)

    shapes = [
        rim_shape(side, c1),
        rim_shape(mid, c1),
        rim_shape(low, c2),
        rim_shape(low, c3),
        rim_shape(low, c3),
        rim_shape(mid, c2),
        rim_shape(side, c1),
        rim_shape(mid, c2),
    ]
    vmem = pl.BlockSpec(memory_space=pltpu.VMEM)
    smem = pl.BlockSpec(memory_space=pltpu.SMEM)
    result = pl.pallas_call(
        functools.partial(kernel, faces, patches, (side, c1, c2, c3)),
        out_shape=jax.ShapeDtypeStruct((c1, count), BF16),
        in_specs=[vmem] * 13 + [smem] * 3,
        out_specs=vmem,
        scratch_shapes=[
            padded(side),
            padded(mid),
            padded(mid),
            padded(low),
            pltpu.VMEM((count, 128), F32),
            pltpu.VMEM((count // 4, 128), F32),
            pltpu.VMEM((count // 16, 128), F32),
            pltpu.VMEM((count // 4, 128), F32),
            pltpu.VMEM((count, 128), F32),
            pltpu.VMEM((count // 4, 128), F32),
            pltpu.VMEM((4 * (side + 2 * SIDE_GAP), 128), F32),
            pltpu.VMEM((4 * (side + 2 * SIDE_GAP), 128), F32),
        ]
        + [
            pltpu.VMEM((9,) + shape, BF16)
            for shape in (
                (c1, c1), (c2, c1), (c3, c2), (c3, c3), (c2, c3), (c2, c2), (c1, c2 + c1)
            )
        ]
        + [pltpu.VMEM((4,) + shape, BF16) for shape in shapes]
        + [pltpu.VMEM((places,) + shape, BF16) for shape in shapes]
        + [
            pltpu.SemaphoreType.DMA((3, 8)),
            pltpu.SemaphoreType.DMA((3, 2, shifts, outers)),
            pltpu.SemaphoreType.DMA((8, places)),
        ],
        compiler_params=pltpu.CompilerParams(
            collective_id=0, has_side_effects=True, vmem_limit_bytes=56 * 1024 * 1024
        ),
    )(
        features[:, 0, :],
        f1, f2, f3, f4, f5, f6,
        w1, w2, w3, w4, w5, w6,
        *(table.transpose(0, 2, 1) for table in tables),
    )
    return result[:, None, :]


def solution(mesh):
    spec = P(None, "face", "patch")
    return jax.shard_map(
        functools.partial(body, mesh.shape["face"], mesh.shape["patch"]),
        mesh=mesh,
        in_specs=(spec,) + (P(),) * 15,
        out_specs=spec,
        check_vma=False,
    )
```

```python
import functools
import math

import jax
import jax.numpy as jnp
from jax import lax
from jax.experimental import pallas as pl
from jax.experimental.pallas import tpu as pltpu
from jax.sharding import PartitionSpec as P

EPSILON = 1e-05
FLOOR_SQUARE = 0.5
MESH = pl.DeviceIdType.MESH
F32 = jnp.float32
BF16 = jnp.bfloat16

STEPS = ((-1, 0), (1, 0), (0, -1), (0, 1), (-1, -1), (-1, 1), (1, -1), (1, 1))
OPPOSITE = (1, 0, 3, 2, 7, 6, 5, 4)
READ_EDGE = (1, 0, 3, 2, 1, 1, 0, 0)
READ_LAST = (None, None, None, None, 1, 0, 1, 0)
SIDE_GAP = 8


def turned_source(edge, turns):
    flip = 0
    for _ in range(turns):
        if edge >= 2:
            flip ^= 1
        edge = (3, 2, 0, 1)[edge]
    return edge, flip


def corner_cell(direction, turns):
    edge, flip = turned_source(READ_EDGE[direction], turns)
    last = READ_LAST[direction] ^ flip
    return ((0, last), (1, last), (last, 0), (last, 1))[edge]


def pick(index, options):
    result = jnp.int32(options[0])
    for count in range(1, len(options)):
        result = jnp.where(index == count, jnp.int32(options[count]), result)
    return result


def grid_of(patches):
    rows = 1 << ((patches.bit_length() - 1) // 2)
    return rows, patches // rows


def pack_of(length, channels):
    return max(1, min(length // 16, 128 // channels))


def rim_shape(length, channels):
    count = pack_of(length, channels)
    return (length // count, channels * count)


def pack(edge):
    length, channels = edge.shape
    count = pack_of(length, channels)
    if count == 1:
        return edge
    step = length // count
    return jnp.concatenate([edge[i * step : (i + 1) * step] for i in range(count)], axis=1)


def unpack(rim, length, channels):
    count = pack_of(length, channels)
    if count == 1:
        return rim
    return jnp.concatenate([rim[:, i * channels : (i + 1) * channels] for i in range(count)], axis=0)


def activated(parts, films):
    channels = sum(part.shape[1] for part in parts)
    total = sum(jnp.sum(part * part, axis=1, keepdims=True) for part in parts)
    mean_square = total * (1.0 / channels)
    if channels >= 64:
        inverse = lax.rsqrt(mean_square + EPSILON)
    else:
        inverse = lax.rsqrt(jnp.maximum(mean_square, FLOOR_SQUARE))
    results = []
    for part, (scale, shift) in zip(parts, films):
        shaped = part * inverse * scale + shift
        results.append(shaped / (1.0 + jnp.exp(-shaped)))
    return results


def kernel(faces, patches, sizes, *refs):
    rows, cols = grid_of(patches)
    slots = 2 * (rows + cols)
    outers = 2 * cols + 2 * (rows - 2)
    shifts = 1 if faces == 2 else 2
    side, c1, c2, c3 = sizes
    mid, low = side // 2, side // 4
    (feat, f1, f2, f3, f4, f5, f6, w1, w2, w3, w4, w5, w6, link_patch, link_shift, link_turn, out) = refs[:17]
    scratch = refs[17:]
    p1, p2a, p2b, p3, keep1, keep2, keep3, up2, up1, mid5, ring, ring_b = scratch[:12]
    t1, t2, t3, t4, t5a, t5b, t6 = scratch[12:19]
    rims, landed = scratch[19:27], scratch[27:35]
    near_send, far_send, recv = scratch[35:]

    face = lax.axis_index("face")
    me = lax.axis_index("patch")
    row, col = me // cols, me % cols
    top, bottom, left, right = row == 0, row == rows - 1, col == 0, col == cols - 1
    upright, across = jnp.logical_or(top, bottom), jnp.logical_or(left, right)
    outer = jnp.logical_or(upright, across)
    inside = []
    for dr, dc in STEPS:
        r, c = row + dr, col + dc
        inside.append(
            jnp.logical_and(
                jnp.logical_and(r >= 0, r < rows), jnp.logical_and(c >= 0, c < cols)
            )
        )

    outer_patches = [
        p
        for p in range(patches)
        if p // cols in (0, rows - 1) or p % cols in (0, cols - 1)
    ]

    def far_face(s):
        return lax.rem(face + (faces - 1 if s == 0 else 1), faces)

    barrier = pltpu.get_barrier_semaphore()
    for d, (dr, dc) in enumerate(STEPS):

        @pl.when(inside[d])
        def _(dr=dr, dc=dc):
            pl.semaphore_signal(
                barrier, inc=1, device_id=(face, me + dr * cols + dc), device_id_type=MESH
            )

    @pl.when(outer)
    def _():
        for s in range(shifts):

            for p in outer_patches:
                pl.semaphore_signal(
                    barrier, inc=1, device_id=(far_face(s), p), device_id_type=MESH
                )

    def meet():
        peers = sum(jnp.where(there, 1, 0) for there in inside)
        pl.semaphore_wait(barrier, peers + jnp.where(outer, outers * shifts, 0))

    where_from = []
    for d in range(8):
        q = link_patch[face, d, me]
        shift = link_shift[face, d, me]
        turn = link_turn[face, d, me]
        q_row, q_col = q // cols, q % cols
        if d < 4:
            edge = pick(turn, [turned_source(READ_EDGE[d], t)[0] for t in range(4)])
            flip = pick(turn, [turned_source(READ_EDGE[d], t)[1] for t in range(4)])
        else:
            last_row = pick(turn, [corner_cell(d, t)[0] for t in range(4)])
            last_col = pick(turn, [corner_cell(d, t)[1] for t in range(4)])
            on_row = q_row == last_row * (rows - 1)
            edge = jnp.where(on_row, last_row, 2 + last_col)
            flip = jnp.where(on_row, last_col, last_row)
            flip = jnp.where(shift == 0, jnp.int32(READ_LAST[d]), flip)
        slot = jnp.where(
            edge == 0,
            q_col,
            jnp.where(
                edge == 1,
                cols + q_col,
                jnp.where(edge == 2, 2 * cols + q_row, 2 * cols + rows + q_row),
            ),
        )
        group = jnp.where(shift < 0, slots, 0) if shifts == 2 else 0
        where_from.append((jnp.where(shift == 0, d, 8 + group + slot), flip))

    mine = (
        (upright, jnp.where(top, 0, 1), jnp.where(top, col, cols + col)),
        (across, jnp.where(left, 2, 3), jnp.where(left, 2 * cols + row, 2 * cols + rows + row)),
    )

    def near_copy(n, d):
        dr, dc = STEPS[d]
        o = OPPOSITE[d]
        return pltpu.make_async_remote_copy(
            src_ref=rims[n].at[READ_EDGE[o]],
            dst_ref=landed[n].at[o],
            send_sem=near_send.at[max(0, n - 5), d],
            recv_sem=recv.at[n, o],
            device_id=(face, me + dr * cols + dc),
            device_id_type=MESH,
        )

    def start(n):
        for way, (present, edge, slot) in enumerate(mine):

            @pl.when(present)
            def _(way=way, edge=edge, slot=slot):
                for s in range(shifts):
                    for p in outer_patches:
                        pltpu.make_async_remote_copy(
                            src_ref=rims[n].at[edge],
                            dst_ref=landed[n].at[8 + s * slots + slot],
                            send_sem=far_send.at[max(0, n - 5), way],
                            recv_sem=recv.at[n, 8],
                            device_id=(far_face(s), p),
                            device_id_type=MESH,
                        ).start()

        for d in range(8):

            @pl.when(inside[d])
            def _(d=d):
                near_copy(n, d).start()

    def whole(n, count, sem, got):
        span = landed[n].at[pl.ds(8, count)]
        return pltpu.make_async_remote_copy(
            src_ref=span,
            dst_ref=span,
            send_sem=sem,
            recv_sem=got,
            device_id=(face, me),
            device_id_type=MESH,
        )

    def finish(n):
        for way in range(2):

            @pl.when(mine[way][0])
            def _(way=way):
                sem = far_send.at[max(0, n - 5), way]
                whole(n, outers * shifts, sem, recv.at[n, 8]).wait_send()

        for d in range(8):

            @pl.when(inside[d])
            def _(d=d):
                near_copy(n, d).wait_send()

    def arrive(n):
        for d in range(8):

            @pl.when(inside[d])
            def _(d=d):
                near_copy(n, OPPOSITE[d]).wait_recv()

        @pl.when(outer)
        def _():
            whole(n, slots * shifts, far_send.at[0, 0], recv.at[n, 8]).wait_recv()

    def launch(n, ref, base, pitch, length, count):
        spans = (
            pl.ds(base, length),
            pl.ds(base + (length - 1) * pitch, length),
            pl.ds(base, length, pitch),
            pl.ds(base + length - 1, length, pitch),
        )
        for e, span in enumerate(spans):
            rims[n][e] = pack(ref[span, :][:, :count].astype(BF16))
        if n == 0:
            meet()
        start(n)

    def launch_padded(n, ref, length, count):
        pitch = length + 2 * SIDE_GAP
        launch(n, ref, pitch + SIDE_GAP, pitch, length, count)

    def gather(n, target, source_length, length, channels):
        pitch = length + 2 * SIDE_GAP
        ratio = length // source_length
        line = lax.broadcasted_iota(jnp.int32, (length, source_length), 0) // ratio
        cell = lax.broadcasted_iota(jnp.int32, (length, source_length), 1)
        places = (
            pl.ds(SIDE_GAP, length),
            pl.ds(pitch + SIDE_GAP, length),
            pl.ds(2 * pitch + SIDE_GAP, length),
            pl.ds(3 * pitch + SIDE_GAP, length),
            pl.ds(SIDE_GAP - 1, 1),
            pl.ds(SIDE_GAP + length, 1),
            pl.ds(pitch + SIDE_GAP - 1, 1),
            pl.ds(pitch + SIDE_GAP + length, 1),
        )
        for d in range(8):
            place, flip = where_from[d]
            edge = unpack(landed[n][place], source_length, channels)
            if d < 4:
                order = jnp.where(cell == line + flip * (source_length - 1 - 2 * line), 1.0, 0.0)
                value = jnp.dot(order.astype(BF16), edge, preferred_element_type=F32)
            else:
                wide = edge.astype(F32)
                value = jnp.where(flip == 1, wide[source_length - 1 :], wide[:1])
            target[places[d], :channels] = value

    def border(length, fields, target, flat=0):
        pitch = length + 2 * SIDE_GAP
        for ref, count, _ in fields:
            for side_base in (2 * pitch, 3 * pitch):
                for end in (SIDE_GAP - 1, SIDE_GAP + length):
                    ref[pl.ds(side_base + end, 1), :count] = jnp.zeros((1, count), F32)
        spots = (
            (0, pl.ds(0, length), (0, 1, 2)),
            (1, pl.ds((length - 1) * length, length), (6, 7, 8)),
            (2, pl.ds(0, length, length), (0, 3, 6)),
            (3, pl.ds(length - 1, length, length), (2, 5, 8)),
        )
        for part, span, taps in spots:
            total = None
            for ref, count, weight in fields:
                for move, tap in enumerate(taps):
                    block = ref[pl.ds(part * pitch + SIDE_GAP - 1 + move, length), :count]
                    term = lax.dot_general(
                        block.astype(BF16),
                        weight[tap],
                        (((1,), (1 - flat,)), ((), ())),
                        preferred_element_type=F32,
                    )
                    total = term if total is None else total + term
            target[span, :] = target[span, :] + lanes(total)

    def clear(ref, length):
        pitch = length + 2 * SIDE_GAP
        for start in (0, (length + 1) * pitch):
            ref[pl.ds(start, pitch), :] = jnp.zeros((pitch, 128), F32)
        for start in (SIDE_GAP - 1, SIDE_GAP + length):
            ref[pl.ds(pitch + start, length, pitch), :] = jnp.zeros((length, 128), F32)

    def cut(weight, parts):
        width = weight.shape[1] // 9
        start = 0
        for target in parts:
            count = target.shape[2]
            for k in range(9):
                target[k] = weight[:, k * width + start : k * width + start + count]
            start += count

    def put(ref, base, length, count, values):
        pitch = length + 2 * SIDE_GAP
        for i in range(values.shape[0] // length):
            start = pl.multiple_of(base * pitch, 8) + (i + 1) * pitch + SIDE_GAP
            ref[pl.ds(start, length), :count] = values[i * length : (i + 1) * length]

    def conv(base, step, length, fields, flat=0):
        pitch = length + 2 * SIDE_GAP
        total = None
        for ref, count, weight in fields:
            for u in range(3):
                for v in range(3):
                    lines = []
                    for i in range(step):
                        start = pl.multiple_of(base * pitch, 8) + (i + u) * pitch + SIDE_GAP - 1 + v
                        lines.append(ref[pl.ds(start, length), :][:, :count].astype(BF16))
                    block = lines[0] if step == 1 else jnp.concatenate(lines, axis=0)
                    term = lax.dot_general(
                        block,
                        weight[3 * u + v],
                        (((1,), (1 - flat,)), ((), ())),
                        preferred_element_type=F32,
                    )
                    total = term if total is None else total + term
        return total

    def film_of(ref, start, count):
        return (1.0 + ref[0:1, start : start + count], ref[1:2, start : start + count])

    def loop(count, body):
        def run(i, carry):
            body(i)
            return carry

        lax.fori_loop(0, count, run, 0)

    def coarse(ref, base, step, length, count):
        half = length // 2
        lines = []
        for i in range(step):
            start = pl.multiple_of(base * 2 * length, 8) + 2 * i * length
            quad = [
                ref[pl.ds(start + a * length + b, half, 2), :][:, :count]
                for a in range(2)
                for b in range(2)
            ]
            lines.append((quad[0] + quad[1] + (quad[2] + quad[3])) * 0.25)
        return lines[0] if step == 1 else jnp.concatenate(lines, axis=0)

    def spread(ref, base, step, length, values):
        for i in range(step):
            line = values[i * length : (i + 1) * length]
            start = pl.multiple_of(base * 4 * length, 8) + 4 * i * length
            for a in range(2):
                for b in range(2):
                    ref[pl.ds(start + 2 * a * length + b, length, 2), :] = line

    def lanes(values):
        count = values.shape[1]
        if count == 128:
            return values
        return jnp.concatenate([values, jnp.zeros((values.shape[0], 128 - count), F32)], axis=1)

    step = 8
    cells = step * side
    film1 = film_of(f1, 0, c1)

    def enter(i):
        start = pl.multiple_of(i * cells, cells)
        values = feat[:, pl.ds(start, cells)].astype(F32).T
        keep1[pl.ds(start, cells), :c1] = values
        put(p1, i * step, side, c1, activated([values], [film1])[0])

    loop(side // step, enter)
    launch_padded(0, p1, side, c1)
    clear(p1, side)
    cut(w1, [t1])

    def first(i):
        start = pl.multiple_of(i * cells, cells)
        values = conv(i * step, step, side, [(p1, c1, t1)])
        keep1[pl.ds(start, cells), :c1] = keep1[pl.ds(start, cells), :c1] + values

    loop(side // step, first)
    clear(p2a, mid)
    clear(p2b, mid)
    clear(p3, low)
    cut(w2, [t2])
    for k in range(9):
        t3[k] = w3[k * c2 : (k + 1) * c2, :]
    arrive(0)
    gather(0, ring, side, side, c1)
    border(side, [(ring, c1, t1)], keep1)
    finish(0)

    step2 = 8
    cells2 = step2 * mid
    film2 = film_of(f2, 0, c1)

    def shrink(i):
        values = coarse(keep1, i * step2, step2, side, c1)
        put(p2a, i * step2, mid, c1, activated([values], [film2])[0])

    loop(mid // step2, shrink)
    launch_padded(1, p2a, mid, c1)
    launch(6, keep1, 0, side, side, c1)

    def second(i):
        start = pl.multiple_of(i * cells2, cells2)
        keep2[pl.ds(start, cells2), :c2] = conv(i * step2, step2, mid, [(p2a, c1, t2)])

    loop(mid // step2, second)
    cut(w4, [t4])
    arrive(1)
    gather(1, ring, mid, mid, c1)
    border(mid, [(ring, c1, t2)], keep2)
    finish(1)

    put(p3, 0, low, c2, activated([coarse(keep2, 0, low, mid, c2)], [film_of(f3, 0, c2)])[0])
    launch_padded(2, p3, low, c2)
    launch(7, keep2, 0, mid, mid, c2)
    keep3[...] = conv(0, low, low, [(p3, c2, t3)], 1)
    cut(w5, [t5a, t5b])
    arrive(2)
    gather(2, ring, low, low, c2)
    border(low, [(ring, c2, t3)], keep3, 1)
    finish(2)

    put(p3, 0, low, c3, activated([keep3[...]], [film_of(f4, 0, c3)])[0])
    launch_padded(3, p3, low, c3)
    keep3[...] = keep3[...] + conv(0, low, low, [(p3, c3, t4)])
    cut(w6, [t6])
    arrive(3)
    gather(3, ring, low, low, c3)
    border(low, [(ring, c3, t4)], keep3)
    finish(3)

    launch(4, keep3, 0, low, low, c3)
    spread(up2, 0, low, low, keep3[...])
    films5 = [film_of(f5, 0, c3), film_of(f5, c3, c2)]

    def join_middle(i):
        start = pl.multiple_of(i * cells2, cells2)
        skip = keep2[pl.ds(start, cells2), :c2].astype(BF16).astype(F32)
        one, two = activated([up2[pl.ds(start, cells2), :], skip], films5)
        put(p2a, i * step2, mid, c3, one)
        put(p2b, i * step2, mid, c2, two)

    loop(mid // step2, join_middle)

    def fifth(i):
        start = pl.multiple_of(i * cells2, cells2)
        mid5[pl.ds(start, cells2), :c2] = conv(
            i * step2, step2, mid, [(p2a, c3, t5a), (p2b, c2, t5b)]
        )

    loop(mid // step2, fifth)
    arrive(7)
    arrive(4)
    gather(7, ring_b, mid, mid, c2)
    gather(4, ring, low, mid, c3)
    extent = pl.ds(0, 4 * (mid + 2 * SIDE_GAP))
    one, two = activated([ring[extent, :], ring_b[extent, :c2]], films5)
    ring[extent, :] = one
    ring_b[extent, :c2] = two
    border(mid, [(ring, c3, t5a), (ring_b, c2, t5b)], mid5)
    finish(7)
    finish(4)

    launch(5, mid5, 0, mid, mid, c2)

    def widen(i):
        start = pl.multiple_of(i * cells2, cells2)
        spread(up1, i * step2, step2, mid, mid5[pl.ds(start, cells2), :])

    loop(mid // step2, widen)
    film6 = [film_of(f6, 0, c2 + c1)]

    def join_fine(i):
        start = pl.multiple_of(i * cells, cells)
        skip = keep1[pl.ds(start, cells), :c1].astype(BF16).astype(F32)
        values = jnp.concatenate([up1[pl.ds(start, cells), :c2], skip], axis=1)
        put(p1, i * step, side, c2 + c1, activated([values], film6)[0])

    loop(side // step, join_fine)

    def last(i):
        start = pl.multiple_of(i * cells, cells)
        skip = keep1[pl.ds(start, cells), :c1].astype(BF16).astype(F32)
        keep1[pl.ds(start, cells), :c1] = skip + conv(i * step, step, side, [(p1, c2 + c1, t6)])

    loop(side // step, last)
    arrive(6)
    arrive(5)
    gather(6, ring_b, side, side, c1)
    gather(5, ring, mid, side, c2)
    extent = pl.ds(0, 4 * (side + 2 * SIDE_GAP))
    values = jnp.concatenate([ring[extent, :c2], ring_b[extent, :c1]], axis=1)
    ring[extent, : c2 + c1] = activated([values], film6)[0]
    border(side, [(ring, c2 + c1, t6)], keep1)

    def leave(i):
        start = pl.multiple_of(i * cells, cells)
        out[:, pl.ds(start, cells)] = keep1[pl.ds(start, cells), :c1].T.astype(BF16)

    loop(side // step, leave)
    finish(6)
    finish(5)


def body(faces, patches, features, f1, w1, f2, w2, f3, w3, f4, w4, f5, w5, f6, w6, *tables):
    c1, _, count = features.shape
    c2, c3 = w2.shape[0], w3.shape[0]
    side = math.isqrt(count)
    mid, low = side // 2, side // 4
    rows, cols = grid_of(patches)
    slots = 2 * (rows + cols)
    outers = 2 * cols + 2 * (rows - 2)
    shifts = 1 if faces == 2 else 2
    places = 8 + slots * shifts

    def padded(length):
        return pltpu.VMEM(((length + 2) * (length + 2 * SIDE_GAP), 128), F32)

    shapes = [
        rim_shape(side, c1),
        rim_shape(mid, c1),
        rim_shape(low, c2),
        rim_shape(low, c3),
        rim_shape(low, c3),
        rim_shape(mid, c2),
        rim_shape(side, c1),
        rim_shape(mid, c2),
    ]
    vmem = pl.BlockSpec(memory_space=pltpu.VMEM)
    smem = pl.BlockSpec(memory_space=pltpu.SMEM)
    result = pl.pallas_call(
        functools.partial(kernel, faces, patches, (side, c1, c2, c3)),
        out_shape=jax.ShapeDtypeStruct((c1, count), BF16),
        in_specs=[vmem] * 13 + [smem] * 3,
        out_specs=vmem,
        scratch_shapes=[
            padded(side),
            padded(mid),
            padded(mid),
            padded(low),
            pltpu.VMEM((count, 128), F32),
            pltpu.VMEM((count // 4, 128), F32),
            pltpu.VMEM((count // 16, 128), F32),
            pltpu.VMEM((count // 4, 128), F32),
            pltpu.VMEM((count, 128), F32),
            pltpu.VMEM((count // 4, 128), F32),
            pltpu.VMEM((4 * (side + 2 * SIDE_GAP), 128), F32),
            pltpu.VMEM((4 * (side + 2 * SIDE_GAP), 128), F32),
        ]
        + [
            pltpu.VMEM((9,) + shape, BF16)
            for shape in (
                (c1, c1), (c2, c1), (c2, c3), (c3, c3), (c2, c3), (c2, c2), (c1, c2 + c1)
            )
        ]
        + [pltpu.VMEM((4,) + shape, BF16) for shape in shapes]
        + [pltpu.VMEM((places,) + shape, BF16) for shape in shapes]
        + [
            pltpu.SemaphoreType.DMA((3, 8)),
            pltpu.SemaphoreType.DMA((3, 2)),
            pltpu.SemaphoreType.DMA((8, 9)),
        ],
        compiler_params=pltpu.CompilerParams(
            collective_id=0, has_side_effects=True, vmem_limit_bytes=56 * 1024 * 1024
        ),
    )(
        features[:, 0, :],
        f1, f2, f3, f4, f5, f6,
        w1, w2, w3.T, w4, w5, w6,
        *(table.transpose(0, 2, 1) for table in tables),
    )
    return result[:, None, :]


def solution(mesh):
    spec = P(None, "face", "patch")
    return jax.shard_map(
        functools.partial(body, mesh.shape["face"], mesh.shape["patch"]),
        mesh=mesh,
        in_specs=(spec,) + (P(),) * 15,
        out_specs=spec,
        check_vma=False,
    )
```
